32 devices in a mesh: sec: 4 (over z), tile: 4 (over y, core), role: 2 (over x).
Axes of the slice: x: 2, y: 2, z: 4, core: 2. Of those that a mesh axis runs over, the one named last changes fastest.
Arguments:
- pressure: float32 [32, 256, 8192], P(None, 'sec', ('tile', 'role')), may hold values from -6 to 6
- cell_weight: float32 [8192], P(('tile', 'role')), may hold values from 0.25 to 4
- live_cells: int32 [8], replicated, may hold values from 341 to 1024, as said below
- mode_order: int32 [128], replicated, may hold values from 0 to 127, each once
Outputs:
- gram: float32 [128, 32, 32], P('sec', ('tile', 'role'))
The draws below stay inside these ranges and needn't reach their ends.
Inputs may be any that keep to these rules, and one draw needn't show every extreme that they name: `live_cells`: at least one tile half is full. `mode_order`: each wavenumber appears once.
All inputs are finite; a program needn't handle non-finite values.
Results may differ from the reference program's by a relative error of at most 0.0003.
Values sent between devices are 32-bit elements; how exact they have to be, the bound alone decides.
A program may use at most 128 MiB of HBM per device.

```python
import math
import jax
import jax.numpy as jnp
from jax import lax

NS = 32
THETA = 256
NF = 16
MODES = 128
GCELLS = 1024
GROUPS = 8
CELLS = 8192


def draw_live_cells(key, part):
    counts = jax.random.randint(jax.random.fold_in(key, 11), (GROUPS,), GCELLS // 3, GCELLS + 1)
    chosen = jax.random.randint(jax.random.fold_in(key, 12), (), 0, GROUPS)
    return jnp.where(jnp.arange(GROUPS) == chosen, GCELLS, counts).astype(jnp.int32)


def block_scale(rng, shape, cuts, low, top_value):
    level = 1.0
    for axis_at, shards_of in cuts:
        draws = jax.random.uniform(jax.random.fold_in(jax.random.fold_in(rng, 6), axis_at), (shards_of,), jnp.float32, low / len(cuts), top_value / len(cuts))
        level = level * jnp.repeat(jnp.exp(draws), shape[axis_at] // shards_of).reshape((-1,) + (1,) * (len(shape) - 1 - axis_at))
    return level


def normal_values(rng, extent, scale, most, cuts=(), kind=jnp.bfloat16):
    array = scale * jax.random.normal(rng, extent, jnp.float32)
    if cuts:
        array = array * block_scale(rng, extent, cuts, -0.22, 0.18)
    return jnp.clip(array, -most, most).astype(kind)


def setup_inputs(seed: int = 0) -> dict:
    key_of = jax.random.split(jax.random.key(seed), 5)
    return {
        "pressure": normal_values(key_of[0], (NS, THETA, CELLS), 1.0, 6.0, ((1, 4), (2, 8)), jnp.float32),
        "cell_weight": jnp.clip(jnp.exp(math.log(4.0) - 2.7725887 * jax.random.uniform(key_of[1], (CELLS,), jnp.float32) ** block_scale(key_of[1], (CELLS,), ((0, 8),), -0.2, 0.2)), 0.25, 4.0),
        "live_cells": draw_live_cells(jax.random.fold_in(key_of[4], 71), 0),
        "mode_order": jax.random.permutation(key_of[3], MODES).astype(jnp.int32),
    }


def time_table(count):
    steps = jnp.arange(count, dtype=jnp.int32)
    half = count // 2
    freqs = jnp.arange(half, dtype=jnp.int32)
    hann = 0.5 - 0.5 * jnp.cos(2.0 * math.pi * steps.astype(jnp.float32) / count)
    phase = 2.0 * math.pi * (freqs[:, None] * steps[None, :] % count).astype(jnp.float32) / count
    factor = math.sqrt(8.0 / (3.0 * count))
    return jnp.concatenate([factor * hann[None, :] * jnp.cos(phase), -factor * hann[None, :] * jnp.sin(phase)], axis=0)

def angle_table(mode_order, angles):
    index = jnp.arange(angles, dtype=jnp.int32)
    phase = 2.0 * math.pi * (mode_order[:, None] * index[None, :] % angles).astype(jnp.float32) / angles
    cosine = jnp.cos(phase) / math.sqrt(angles)
    sine = jnp.sin(phase) / math.sqrt(angles)
    return jnp.stack([jnp.stack([cosine, sine], axis=1), jnp.stack([-sine, cosine], axis=1)], axis=0)

def reference(pressure, cell_weight, live_cells, mode_order):
    hi = lax.Precision.HIGHEST
    htab = time_table(NS)
    atab = angle_table(mode_order, THETA)

    def one_group(group):
        start = (group * GCELLS).astype(jnp.int32)
        block = lax.dynamic_slice_in_dim(pressure, start, GCELLS, 2)
        weights = lax.dynamic_slice_in_dim(cell_weight, start, GCELLS, 0)
        live = lax.dynamic_slice_in_dim(live_cells, group.astype(jnp.int32), 1, 0)[0]
        spectra = jnp.einsum('rt,tqc->rqc', htab, block, precision=hi)
        split = spectra.reshape(2, NF, THETA, GCELLS)
        modal = jnp.einsum('okiq,ifqc->kofc', atab, split, precision=hi).reshape(MODES, NS, GCELLS)
        position = jnp.arange(GCELLS, dtype=jnp.int32)
        weighted = jnp.where(position < live, weights / CELLS, jnp.float32(0.0))
        return jnp.einsum('kac,kbc->kab', modal * weighted[None, None, :], modal, precision=hi)
    parts = lax.map(one_group, jnp.arange(GROUPS, dtype=jnp.int32))
    return lax.optimization_barrier(jnp.sum(parts, axis=0))
```

```python
import functools
import math

import jax
import jax.numpy as jnp
from jax import lax
from jax.experimental import pallas as pl
from jax.experimental.pallas import tpu as pltpu
from jax.sharding import PartitionSpec as P

MESH = pl.DeviceIdType.MESH
LANES = 128
SUB = 8
F32 = jnp.float32
BF16 = jnp.bfloat16


def halves(x):
    hi = x.astype(BF16)
    lo = (x - hi.astype(F32)).astype(BF16)
    return hi, lo


def left_terms(x):
    hi, lo = halves(x)
    return jnp.concatenate([hi, hi, lo], axis=1)


def right_terms(x):
    hi, lo = halves(x)
    return jnp.concatenate([hi, lo, hi], axis=0)


def dot(a, b, dims=(((1,), (0,)), ((), ()))):
    return lax.dot_general(a, b, dims, preferred_element_type=F32)


def by_distance(i, me, n):
    right = n - 1 - me
    both = jnp.minimum(me, right)
    paired = i <= 2 * both
    delta = jnp.where(paired, (i + 1) // 2, i - both)
    up = jnp.where(paired, i % 2 == 1, me < right)
    return jnp.where(up, me + delta, me - delta)


def iota(shape, axis):
    return lax.broadcasted_iota(jnp.int32, shape, axis)


def time_terms(snaps):
    size = snaps * SUB
    row, col = iota((size, size), 0), iota((size, size), 1)
    half = snaps // 2
    r, t = row // SUB, col // SUB
    f = r % half
    hann = 0.5 - 0.5 * jnp.cos((2.0 * math.pi / snaps) * t.astype(F32))
    phase = (2.0 * math.pi / snaps) * ((f * t) % snaps).astype(F32)
    wave = jnp.where(r < half, jnp.cos(phase), -jnp.sin(phase))
    value = math.sqrt(8.0 / (3.0 * snaps)) * hann * wave
    return jnp.where(row % SUB == col % SUB, value, 0.0)


def angle_terms(modes_row, angles):
    modes = modes_row.shape[1]
    index = iota((angles, modes), 0)
    phase = (2.0 * math.pi / angles) * ((modes_row * index) % angles).astype(F32)
    scale = 1.0 / math.sqrt(angles)
    return jnp.concatenate([(jnp.cos(phase) * scale).T, (jnp.sin(phase) * scale).T], axis=0)


def kernel(n_sec, n_tile, n_role, p_ref, w_ref, live_ref, mode_ref, out_ref,
           recv, spec, zbuf, acc, reda, sb, redb, ttab, atab,
           send_sem, recv_sem, own_sem, sa_sem, ra_sem, sb_sem, rb_sem):
    me = lax.axis_index("sec")
    tile, role = lax.axis_index("tile"), lax.axis_index("role")
    n_grp = n_tile * n_role
    grp = tile * n_role + role
    snaps, q_loc, cells = p_ref.shape
    half = snaps // 2
    angles = q_loc * n_sec
    modes = mode_ref.shape[1]
    cell_dev = cells // n_sec
    subs = cell_dev // LANES
    pack = LANES // snaps
    part = snaps // n_grp

    def peer(o):
        other = lax.rem(grp + o, n_grp)
        return other, {"tile": other // n_role, "role": other % n_role}

    barrier = pltpu.get_barrier_semaphore()
    for o in range(1, n_sec):
        pl.semaphore_signal(barrier, inc=1, device_id={"sec": lax.rem(me + o, n_sec)}, device_id_type=MESH)
    for o in range(1, n_grp):
        pl.semaphore_signal(barrier, inc=1, device_id=peer(o)[1], device_id_type=MESH)
    pl.semaphore_wait(barrier, n_sec + n_grp - 2)

    def piece(owner, j):
        start = pl.multiple_of(owner * cell_dev + j * LANES, LANES)
        return p_ref.at[:, :, pl.ds(start, LANES)]

    def outgoing(i, j):
        dest = by_distance(i, me, n_sec)
        return pltpu.make_async_remote_copy(
            src_ref=piece(dest, j), dst_ref=recv.at[j, me],
            send_sem=send_sem.at[j, dest], recv_sem=recv_sem.at[j, me],
            device_id={"sec": dest}, device_id_type=MESH)

    def own(j):
        return pltpu.make_async_copy(piece(me, j), recv.at[j, me], own_sem.at[j])

    for j in range(subs):
        @pl.loop(1, n_sec)
        def _(i):
            outgoing(i, j).start()
    for j in range(subs):
        own(j).start()

    ttab[...] = left_terms(time_terms(snaps))
    atab[...] = left_terms(angle_terms(mode_ref[...], angles))
    live = live_ref[grp]
    total = float(cells * n_grp)
    wide = 2 if q_loc % (2 * SUB) == 0 else 1

    def to_spectra(j, src):
        for g in range(0, q_loc, wide * SUB):
            x = jnp.concatenate(
                [recv[j, src, :, g + u * SUB:g + (u + 1) * SUB, :].reshape(snaps * SUB, LANES) for u in range(wide)],
                axis=1)
            y = dot(ttab[...], right_terms(x))
            for u in range(wide):
                at = pl.multiple_of(src * q_loc + g + u * SUB, SUB)
                spec[:, pl.ds(at, SUB), :] = y[:, u * LANES:(u + 1) * LANES].reshape(snaps, SUB, LANES)

    for j in range(subs):
        own(j).wait()
        to_spectra(j, me)

        @pl.loop(1, n_sec)
        def _(i):
            src = by_distance(i, me, n_sec)
            pltpu.make_async_remote_copy(
                src_ref=recv.at[j, src], dst_ref=recv.at[j, src],
                send_sem=send_sem.at[j, src], recv_sem=recv_sem.at[j, src],
                device_id={"sec": src}, device_id_type=MESH).wait_recv()
            to_spectra(j, src)

        @pl.loop(0, half)
        def _(f):
            x = jnp.concatenate([spec[f], spec[half + f]], axis=1)
            y = dot(atab[...], right_terms(x))
            zbuf[pl.ds(f, modes, stride=snaps), :] = y[:modes, :LANES] + y[modes:, LANES:]
            zbuf[pl.ds(half + f, modes, stride=snaps), :] = y[:modes, LANES:] - y[modes:, :LANES]

        first = pl.multiple_of(me * cell_dev + j * LANES, LANES)
        position = first + iota((1, LANES), 1)
        weight = jnp.where(position < live, w_ref[:, pl.ds(first, LANES)] / total, 0.0)
        block = iota((snaps, LANES), 1) // snaps
        steps = SUB // part

        @pl.loop(0, modes // pack // steps)
        def _(h):
            rows = []
            for u in range(steps):
                at = pl.multiple_of((h * steps + u) * LANES, LANES)
                z = zbuf[pl.ds(at, LANES), :]
                zh, zl = halves(z)
                g4 = dot(left_terms(z * weight), jnp.concatenate([zh, zl, zh], axis=1), (((1,), (1,)), ((), ())))
                r = g4[:snaps]
                for b in range(1, pack):
                    r = jnp.where(block == b, g4[b * snaps:(b + 1) * snaps], r)
                rows.append(r)
            at = pl.multiple_of(h * SUB, SUB)
            for g in range(n_grp):
                new = jnp.concatenate([r[g * part:(g + 1) * part] for r in rows], axis=0)
                if j == 0:
                    acc[g, pl.ds(at, SUB), :] = new
                else:
                    acc[g, pl.ds(at, SUB), :] += new

    def share(o):
        other, device = peer(o)
        return pltpu.make_async_remote_copy(
            src_ref=acc.at[other], dst_ref=reda.at[grp],
            send_sem=sa_sem.at[other], recv_sem=ra_sem.at[grp],
            device_id=device, device_id_type=MESH)

    def shared(o):
        other, device = peer(o)
        return pltpu.make_async_remote_copy(
            src_ref=acc.at[other], dst_ref=reda.at[other],
            send_sem=sa_sem.at[other], recv_sem=ra_sem.at[other],
            device_id=device, device_id_type=MESH)

    for o in range(1, n_grp):
        share(o).start()
    for o in range(1, n_grp):
        shared(o).wait_recv()
    rows = sb.shape[1]
    for s in range(n_sec):
        value = acc[grp, s * rows:(s + 1) * rows, :]
        for o in range(1, n_grp):
            value += reda[peer(o)[0], s * rows:(s + 1) * rows, :]
        sb[s] = value

    def last(s, slot):
        return pltpu.make_async_remote_copy(
            src_ref=sb.at[s], dst_ref=redb.at[slot],
            send_sem=sb_sem.at[s], recv_sem=rb_sem.at[slot],
            device_id={"sec": s}, device_id_type=MESH)

    for o in range(1, n_sec):
        last(lax.rem(me + o, n_sec), me).start()
    value = sb[me]
    for o in range(1, n_sec):
        s = lax.rem(me + o, n_sec)
        last(s, s).wait_recv()
        value += redb[s]
    out_ref[...] = value

    for j in range(subs):
        @pl.loop(1, n_sec)
        def _(i):
            outgoing(i, j).wait_send()
    for o in range(1, n_grp):
        share(o).wait_send()
    for o in range(1, n_sec):
        last(lax.rem(me + o, n_sec), me).wait_send()


def on_device(pressure, cell_weight, live_cells, mode_order):
    n_sec, n_tile, n_role = (lax.axis_size(a) for a in ("sec", "tile", "role"))
    n_grp = n_tile * n_role
    snaps, q_loc, cells = pressure.shape
    modes = mode_order.shape[0]
    angles = q_loc * n_sec
    subs = cells // n_sec // LANES
    pack = LANES // snaps
    part = snaps // n_grp
    rows = modes // pack * part
    own_rows = rows // n_sec
    vmem = pl.BlockSpec(memory_space=pltpu.VMEM)
    dma = pltpu.SemaphoreType.DMA
    packed = pl.pallas_call(
        functools.partial(kernel, n_sec, n_tile, n_role),
        out_shape=jax.ShapeDtypeStruct((own_rows, LANES), F32),
        in_specs=[pl.BlockSpec(memory_space=pl.ANY), vmem, pl.BlockSpec(memory_space=pltpu.SMEM), vmem],
        out_specs=vmem,
        scratch_shapes=[
            pltpu.VMEM((subs, n_sec, snaps, q_loc, LANES), F32),
            pltpu.VMEM((snaps, angles, LANES), F32),
            pltpu.VMEM((modes * snaps, LANES), F32),
            pltpu.VMEM((n_grp, rows, LANES), F32),
            pltpu.VMEM((n_grp, rows, LANES), F32),
            pltpu.VMEM((n_sec, own_rows, LANES), F32),
            pltpu.VMEM((n_sec, own_rows, LANES), F32),
            pltpu.VMEM((snaps * SUB, 3 * snaps * SUB), BF16),
            pltpu.VMEM((2 * modes, 3 * angles), BF16),
            dma((subs, n_sec)), dma((subs, n_sec)), dma((subs,)),
            dma((n_grp,)), dma((n_grp,)), dma((n_sec,)), dma((n_sec,)),
        ],
        compiler_params=pltpu.CompilerParams(
            collective_id=0, has_side_effects=True, vmem_limit_bytes=60 * 2**20),
        name="spod",
    )(pressure, cell_weight.reshape(1, cells), live_cells, mode_order.reshape(1, modes))
    out = packed.reshape(modes // pack // n_sec, part, pack, snaps)
    return out.transpose(0, 2, 1, 3).reshape(modes // n_sec, part, snaps)


def solution(mesh):
    in_specs = (P(None, "sec", ("tile", "role")), P(("tile", "role")), P(), P())
    out_specs = P("sec", ("tile", "role"), None)
    return jax.shard_map(
        on_device, mesh=mesh, in_specs=in_specs, out_specs=out_specs, check_vma=False
    )
```

```python
import functools
import math

import jax
import jax.numpy as jnp
from jax import lax
from jax.experimental import pallas as pl
from jax.experimental.pallas import tpu as pltpu
from jax.sharding import PartitionSpec as P

MESH = pl.DeviceIdType.MESH
LANES = 128
UNROLL = 4
STAGES = 4
SUB = 8
F32 = jnp.float32
BF16 = jnp.bfloat16


def halves(x):
    hi = x.astype(BF16)
    lo = (x - hi.astype(F32)).astype(BF16)
    return hi, lo


def left_terms(x):
    hi, lo = halves(x)
    return jnp.concatenate([hi, hi, lo], axis=1)


def right_terms(x):
    hi, lo = halves(x)
    return jnp.concatenate([hi, lo, hi], axis=0)


def dot(a, b, dims=(((1,), (0,)), ((), ()))):
    return lax.dot_general(a, b, dims, preferred_element_type=F32)


def partner(i, me, n):
    x = jnp.where(i == 1, n - 1, i - 1)
    other, bit = 0, 1
    while bit < n:
        other += (me // bit + x // bit) % 2 * bit
        bit *= 2
    return other


def iota(shape, axis):
    return lax.broadcasted_iota(jnp.int32, shape, axis)


def time_terms(snaps):
    size = snaps * SUB
    row, col = iota((size, size), 0), iota((size, size), 1)
    half = snaps // 2
    r, t = row // SUB, col // SUB
    f = r % half
    hann = 0.5 - 0.5 * jnp.cos((2.0 * math.pi / snaps) * t.astype(F32))
    phase = (2.0 * math.pi / snaps) * ((f * t) % snaps).astype(F32)
    wave = jnp.where(r < half, jnp.cos(phase), -jnp.sin(phase))
    value = math.sqrt(8.0 / (3.0 * snaps)) * hann * wave
    return jnp.where(row % SUB == col % SUB, value, 0.0)


def angle_terms(modes_row, angles, first, count):
    index = first + iota((count, modes_row.shape[1]), 0)
    phase = (2.0 * math.pi / angles) * ((modes_row * index) % angles).astype(F32)
    scale = 1.0 / math.sqrt(angles)
    return jnp.concatenate([(jnp.cos(phase) * scale).T, (jnp.sin(phase) * scale).T], axis=0)


def kernel(n_sec, n_tile, n_role, p_ref, w_ref, live_ref, mode_ref, out_ref,
           recv, spec, zbuf, acc, reda, sb, redb, ttab, atab, ltab, ypart,
           send_sem, recv_sem, own_sem, sa_sem, ra_sem, sb_sem, rb_sem):
    me = lax.axis_index("sec")
    tile, role = lax.axis_index("tile"), lax.axis_index("role")
    n_grp = n_tile * n_role
    grp = tile * n_role + role
    snaps, q_loc, cells = p_ref.shape
    half = snaps // 2
    angles = q_loc * n_sec
    modes = mode_ref.shape[1]
    cell_dev = cells // n_sec
    subs = cell_dev // LANES
    pack = LANES // snaps
    part = snaps // n_grp
    split = q_loc % 16 == 0

    def peer(o):
        other = lax.rem(grp + o, n_grp)
        return other, {"tile": other // n_role, "role": other % n_role}

    barrier = pltpu.get_barrier_semaphore()
    for o in range(1, n_sec):
        pl.semaphore_signal(barrier, inc=1, device_id={"sec": lax.rem(me + o, n_sec)}, device_id_type=MESH)
    for o in range(1, n_grp):
        pl.semaphore_signal(barrier, inc=1, device_id=peer(o)[1], device_id_type=MESH)
    pl.semaphore_wait(barrier, n_sec + n_grp - 2)

    def piece(owner, j):
        start = pl.multiple_of(owner * cell_dev + j * LANES, LANES)
        return p_ref.at[:, :, pl.ds(start, LANES)]

    def outgoing(i, j):
        dest = partner(i, me, n_sec)
        return pltpu.make_async_remote_copy(
            src_ref=piece(dest, j), dst_ref=recv.at[j, me],
            send_sem=send_sem.at[j, dest], recv_sem=recv_sem.at[j, me],
            device_id={"sec": dest}, device_id_type=MESH)

    def own(j):
        return pltpu.make_async_copy(piece(me, j), recv.at[j, me], own_sem.at[j])

    for j in range(subs):
        @pl.loop(1, n_sec)
        def _(i):
            outgoing(i, j).start()
    for j in range(subs):
        own(j).start()

    ttab[...] = left_terms(time_terms(snaps))
    atab[...] = left_terms(angle_terms(mode_ref[...], angles, 0, angles))
    late = partner(n_sec - 1, me, n_sec)
    late_at = pl.multiple_of(late * q_loc, SUB)
    if split:
        ltab[...] = left_terms(angle_terms(mode_ref[...], angles, late_at, q_loc))
    live = live_ref[grp]
    total = float(cells * n_grp)
    wide = 2 if q_loc % (2 * SUB) == 0 else 1

    def to_spectra(j, src):
        for g in range(0, q_loc, wide * SUB):
            x = jnp.concatenate(
                [recv[j, src, :, g + u * SUB:g + (u + 1) * SUB, :].reshape(snaps * SUB, LANES) for u in range(wide)],
                axis=1)
            y = dot(ttab[...], right_terms(x))
            for u in range(wide):
                at = pl.multiple_of(src * q_loc + g + u * SUB, SUB)
                spec[:, pl.ds(at, SUB), :] = y[:, u * LANES:(u + 1) * LANES].reshape(snaps, SUB, LANES)

    stage_rows = acc.shape[1] // STAGES

    def share(o, t, arriving=False):
        other, device = peer(o)
        at = pl.ds(t * stage_rows, stage_rows)
        slot = other if arriving else grp
        return pltpu.make_async_remote_copy(
            src_ref=acc.at[other, at, :], dst_ref=reda.at[slot, at, :],
            send_sem=sa_sem.at[t, other], recv_sem=ra_sem.at[t, slot],
            device_id=device, device_id_type=MESH)

    def arrive(i, j):
        src = partner(i, me, n_sec)
        pltpu.make_async_remote_copy(
            src_ref=recv.at[j, src], dst_ref=recv.at[j, src],
            send_sem=send_sem.at[j, src], recv_sem=recv_sem.at[j, src],
            device_id={"sec": src}, device_id_type=MESH).wait_recv()
        to_spectra(j, src)

    def to_modal(f, y):
        zbuf[pl.ds(f, modes, stride=snaps), :] = y[:modes, :LANES] + y[modes:, LANES:]
        zbuf[pl.ds(half + f, modes, stride=snaps), :] = y[:modes, LANES:] - y[modes:, :LANES]

    def products(f):
        x = jnp.concatenate([spec[f], spec[half + f]], axis=1)
        return dot(atab[...], right_terms(x))

    for j in range(subs):
        own(j).wait()
        to_spectra(j, me)
        early = split and j == subs - 1

        @pl.loop(1, n_sec - 1 if early else n_sec)
        def _(i):
            arrive(i, j)

        if early:
            spec[:, pl.ds(late_at, q_loc), :] = jnp.zeros((snaps, q_loc, LANES), F32)

            @pl.loop(0, half)
            def _(f):
                ypart[f] = products(f)

            arrive(n_sec - 1, j)

            @pl.loop(0, half, unroll=UNROLL)
            def _(f):
                x = jnp.concatenate([spec[f, pl.ds(late_at, q_loc), :], spec[half + f, pl.ds(late_at, q_loc), :]], axis=1)
                to_modal(f, ypart[f] + dot(ltab[...], right_terms(x)))
        else:
            @pl.loop(0, half, unroll=UNROLL)
            def _(f):
                to_modal(f, products(f))

        first = pl.multiple_of(me * cell_dev + j * LANES, LANES)
        position = first + iota((1, LANES), 1)
        weight = jnp.where(position < live, w_ref[pl.ds(me * subs + j, 1), :] / total, 0.0)
        block = iota((snaps, LANES), 1) // snaps
        steps = SUB // part

        def gram(h):
            rows = []
            for u in range(steps):
                at = pl.multiple_of((h * steps + u) * LANES, LANES)
                z = zbuf[pl.ds(at, LANES), :]
                zh, zl = halves(z)
                g4 = dot(left_terms(z * weight), jnp.concatenate([zh, zl, zh], axis=1), (((1,), (1,)), ((), ())))
                r = g4[:snaps]
                for b in range(1, pack):
                    r = jnp.where(block == b, g4[b * snaps:(b + 1) * snaps], r)
                rows.append(r)
            at = pl.multiple_of(h * SUB, SUB)
            for g in range(n_grp):
                new = jnp.concatenate([r[g * part:(g + 1) * part] for r in rows], axis=0)
                if j == 0:
                    acc[g, pl.ds(at, SUB), :] = new
                else:
                    acc[g, pl.ds(at, SUB), :] += new

        count = modes // pack // steps // STAGES
        for t in range(STAGES):
            pl.loop(t * count, (t + 1) * count, unroll=UNROLL)(gram)
            if j == subs - 1:
                for o in range(1, n_grp):
                    share(o, t).start()

    def last(s, slot):
        return pltpu.make_async_remote_copy(
            src_ref=sb.at[s], dst_ref=redb.at[slot],
            send_sem=sb_sem.at[s], recv_sem=rb_sem.at[slot],
            device_id={"sec": s}, device_id_type=MESH)

    rows = sb.shape[1]
    for t in range(STAGES):
        for o in range(1, n_grp):
            share(o, t, True).wait_recv()
        for s in range(t * n_sec // STAGES, (t + 1) * n_sec // STAGES):
            value = acc[grp, s * rows:(s + 1) * rows, :]
            for o in range(1, n_grp):
                value += reda[peer(o)[0], s * rows:(s + 1) * rows, :]
            sb[s] = value

            @pl.when(me != s)
            def _():
                last(s, me).start()

    value = sb[me]
    for o in range(1, n_sec):
        s = lax.rem(me + o, n_sec)
        last(s, s).wait_recv()
        value += redb[s]
    out_ref[...] = value

    for j in range(subs):
        @pl.loop(1, n_sec)
        def _(i):
            outgoing(i, j).wait_send()
    for t in range(STAGES):
        for o in range(1, n_grp):
            share(o, t).wait_send()
    for o in range(1, n_sec):
        last(lax.rem(me + o, n_sec), me).wait_send()


def on_device(pressure, cell_weight, live_cells, mode_order):
    n_sec, n_tile, n_role = (lax.axis_size(a) for a in ("sec", "tile", "role"))
    n_grp = n_tile * n_role
    snaps, q_loc, cells = pressure.shape
    modes = mode_order.shape[0]
    angles = q_loc * n_sec
    subs = cells // n_sec // LANES
    pack = LANES // snaps
    part = snaps // n_grp
    rows = modes // pack * part
    own_rows = rows // n_sec
    vmem = pl.BlockSpec(memory_space=pltpu.VMEM)
    dma = pltpu.SemaphoreType.DMA
    packed = pl.pallas_call(
        functools.partial(kernel, n_sec, n_tile, n_role),
        out_shape=jax.ShapeDtypeStruct((own_rows, LANES), F32),
        in_specs=[pl.BlockSpec(memory_space=pl.ANY), vmem, pl.BlockSpec(memory_space=pltpu.SMEM), vmem],
        out_specs=vmem,
        scratch_shapes=[
            pltpu.VMEM((subs, n_sec, snaps, q_loc, LANES), F32),
            pltpu.VMEM((snaps, angles, LANES), F32),
            pltpu.VMEM((modes * snaps, LANES), F32),
            pltpu.VMEM((n_grp, rows, LANES), F32),
            pltpu.VMEM((n_grp, rows, LANES), F32),
            pltpu.VMEM((n_sec, own_rows, LANES), F32),
            pltpu.VMEM((n_sec, own_rows, LANES), F32),
            pltpu.VMEM((snaps * SUB, 3 * snaps * SUB), BF16),
            pltpu.VMEM((2 * modes, 3 * angles), BF16),
            pltpu.VMEM((2 * modes, 3 * q_loc), BF16),
            pltpu.VMEM((snaps // 2, 2 * modes, 2 * LANES), F32),
            dma((subs, n_sec)), dma((subs, n_sec)), dma((subs,)),
            dma((STAGES, n_grp)), dma((STAGES, n_grp)), dma((n_sec,)), dma((n_sec,)),
        ],
        compiler_params=pltpu.CompilerParams(
            collective_id=0, has_side_effects=True, vmem_limit_bytes=60 * 2**20),
        name="spod",
    )(pressure, cell_weight.reshape(cells // LANES, LANES), live_cells, mode_order.reshape(1, modes))
    out = packed.reshape(modes // pack // n_sec, part, pack, snaps)
    return out.transpose(0, 2, 1, 3).reshape(modes // n_sec, part, snaps)


def solution(mesh):
    in_specs = (P(None, "sec", ("tile", "role")), P(("tile", "role")), P(), P())
    out_specs = P("sec", ("tile", "role"), None)
    return jax.shard_map(
        on_device, mesh=mesh, in_specs=in_specs, out_specs=out_specs, check_vma=False
    )
```

```python
import functools
import math

import jax
import jax.numpy as jnp
from jax import lax
from jax.experimental import pallas as pl
from jax.experimental.pallas import tpu as pltpu
from jax.sharding import PartitionSpec as P

MESH = pl.DeviceIdType.MESH
LANES = 128
UNROLL = 4
STAGES = 4
SUB = 8
F32 = jnp.float32
BF16 = jnp.bfloat16


def halves(x):
    hi = x.astype(BF16)
    lo = (x - hi.astype(F32)).astype(BF16)
    return hi, lo


def left_terms(x):
    hi, lo = halves(x)
    return jnp.concatenate([hi, hi, lo], axis=1)


def right_terms(x):
    hi, lo = halves(x)
    return jnp.concatenate([hi, lo, hi], axis=0)


def dot(a, b, dims=(((1,), (0,)), ((), ()))):
    return lax.dot_general(a, b, dims, preferred_element_type=F32)


def partner(x, me, n):
    other, bit = 0, 1
    while bit < n:
        other += (me // bit + x // bit) % 2 * bit
        bit *= 2
    return other


def iota(shape, axis):
    return lax.broadcasted_iota(jnp.int32, shape, axis)


def time_terms(snaps):
    size = snaps * SUB
    row, col = iota((size, size), 0), iota((size, size), 1)
    half = snaps // 2
    r, t = row // SUB, col // SUB
    f = r % half
    hann = 0.5 - 0.5 * jnp.cos((2.0 * math.pi / snaps) * t.astype(F32))
    phase = (2.0 * math.pi / snaps) * ((f * t) % snaps).astype(F32)
    wave = jnp.where(r < half, jnp.cos(phase), -jnp.sin(phase))
    value = math.sqrt(8.0 / (3.0 * snaps)) * hann * wave
    return jnp.where(row % SUB == col % SUB, value, 0.0)


def angle_terms(modes_row, angles, first, count):
    index = first + iota((count, modes_row.shape[1]), 0)
    phase = (2.0 * math.pi / angles) * ((modes_row * index) % angles).astype(F32)
    scale = 1.0 / math.sqrt(angles)
    return jnp.concatenate([(jnp.cos(phase) * scale).T, (jnp.sin(phase) * scale).T], axis=0)


def kernel(n_sec, n_tile, n_role, p_ref, w_ref, live_ref, mode_ref, out_ref,
           recv, spec, zbuf, acc, pbuf, pacc, reda, sb, redb, ttab, atab, ltab, ypart,
           send_sem, recv_sem, own_sem, pa_sem, pr_sem, sa_sem, ra_sem, sb_sem, rb_sem):
    me = lax.axis_index("sec")
    tile, role = lax.axis_index("tile"), lax.axis_index("role")
    n_grp = n_tile * n_role
    grp = tile * n_role + role
    near = n_grp // 2
    side, mine = tile % 2, tile // 2 * n_role + role
    snaps, q_loc, cells = p_ref.shape
    half = snaps // 2
    angles = q_loc * n_sec
    modes = mode_ref.shape[1]
    cell_dev = cells // n_sec
    subs = cell_dev // LANES
    pack = LANES // snaps
    part = snaps // n_grp
    split = q_loc % 16 == 0

    def peer(o):
        other = lax.rem(grp + o, n_grp)
        return other, {"tile": other // n_role, "role": other % n_role}

    barrier = pltpu.get_barrier_semaphore()
    for o in range(1, n_sec):
        pl.semaphore_signal(barrier, inc=1, device_id={"sec": lax.rem(me + o, n_sec)}, device_id_type=MESH)
    for o in range(1, n_grp):
        pl.semaphore_signal(barrier, inc=1, device_id=peer(o)[1], device_id_type=MESH)
    pl.semaphore_wait(barrier, n_sec + n_grp - 2)

    def piece(owner, j):
        start = pl.multiple_of(owner * cell_dev + j * LANES, LANES)
        return p_ref.at[:, :, pl.ds(start, LANES)]

    def outgoing(i, j):
        dest = partner(i, me, n_sec)
        return pltpu.make_async_remote_copy(
            src_ref=piece(dest, j), dst_ref=recv.at[j, me],
            send_sem=send_sem.at[j, dest], recv_sem=recv_sem.at[j, me],
            device_id={"sec": dest}, device_id_type=MESH)

    def own(j):
        return pltpu.make_async_copy(piece(me, j), recv.at[j, me], own_sem.at[j])

    for j in range(subs):
        @pl.loop(1, n_sec)
        def _(i):
            outgoing(i, j).start()
    for j in range(subs):
        own(j).start()

    ttab[...] = left_terms(time_terms(snaps))
    atab[...] = left_terms(angle_terms(mode_ref[...], angles, 0, angles))
    late = partner(n_sec - 1, me, n_sec)
    late_at = pl.multiple_of(late * q_loc, SUB)
    if split:
        ltab[...] = left_terms(angle_terms(mode_ref[...], angles, late_at, q_loc))
    live = live_ref[grp]
    total = float(cells * n_grp)
    wide = 2 if q_loc % (2 * SUB) == 0 else 1

    def to_spectra(j, src):
        for g in range(0, q_loc, wide * SUB):
            x = jnp.concatenate(
                [recv[j, src, :, g + u * SUB:g + (u + 1) * SUB, :].reshape(snaps * SUB, LANES) for u in range(wide)],
                axis=1)
            y = dot(ttab[...], right_terms(x))
            for u in range(wide):
                at = pl.multiple_of(src * q_loc + g + u * SUB, SUB)
                spec[:, pl.ds(at, SUB), :] = y[:, u * LANES:(u + 1) * LANES].reshape(snaps, SUB, LANES)

    stage_rows = acc.shape[1] // STAGES

    def pair(t):
        at = pl.ds(t * stage_rows, stage_rows)
        return pltpu.make_async_remote_copy(
            src_ref=acc.at[pl.ds((1 - side) * near, near), at, :], dst_ref=pbuf.at[:, at, :],
            send_sem=pa_sem.at[t], recv_sem=pr_sem.at[t],
            device_id={"tile": tile + 1 - 2 * side}, device_id_type=MESH)

    def share(o, t, arriving=False):
        other = lax.rem(mine + o, near)
        at = pl.ds(t * stage_rows, stage_rows)
        slot = other if arriving else mine
        return pltpu.make_async_remote_copy(
            src_ref=pacc.at[other, at, :], dst_ref=reda.at[slot, at, :],
            send_sem=sa_sem.at[t, other], recv_sem=ra_sem.at[t, slot],
            device_id={"tile": other // n_role * 2 + side, "role": other % n_role}, device_id_type=MESH)

    def forward(t):
        pair(t).wait_recv()
        at = pl.ds(t * stage_rows, stage_rows)
        pacc[:, at, :] = acc[pl.ds(side * near, near), at, :] + pbuf[:, at, :]
        for o in range(1, near):
            share(o, t).start()

    def arrive(i, j):
        src = partner(i, me, n_sec)
        pltpu.make_async_remote_copy(
            src_ref=recv.at[j, src], dst_ref=recv.at[j, src],
            send_sem=send_sem.at[j, src], recv_sem=recv_sem.at[j, src],
            device_id={"sec": src}, device_id_type=MESH).wait_recv()
        to_spectra(j, src)

    def to_modal(f, y):
        zbuf[pl.ds(f, modes, stride=snaps), :] = y[:modes, :LANES] + y[modes:, LANES:]
        zbuf[pl.ds(half + f, modes, stride=snaps), :] = y[:modes, LANES:] - y[modes:, :LANES]

    def products(f):
        x = jnp.concatenate([spec[f], spec[half + f]], axis=1)
        return dot(atab[...], right_terms(x))

    for j in range(subs):
        own(j).wait()
        to_spectra(j, me)
        early = split and j == subs - 1

        @pl.loop(1, n_sec - 1 if early else n_sec)
        def _(i):
            arrive(i, j)

        if early:
            spec[:, pl.ds(late_at, q_loc), :] = jnp.zeros((snaps, q_loc, LANES), F32)

            @pl.loop(0, half)
            def _(f):
                ypart[f] = products(f)

            arrive(n_sec - 1, j)

            @pl.loop(0, half, unroll=UNROLL)
            def _(f):
                x = jnp.concatenate([spec[f, pl.ds(late_at, q_loc), :], spec[half + f, pl.ds(late_at, q_loc), :]], axis=1)
                to_modal(f, ypart[f] + dot(ltab[...], right_terms(x)))
        else:
            @pl.loop(0, half, unroll=UNROLL)
            def _(f):
                to_modal(f, products(f))

        first = pl.multiple_of(me * cell_dev + j * LANES, LANES)
        position = first + iota((1, LANES), 1)
        weight = jnp.where(position < live, w_ref[pl.ds(me * subs + j, 1), :] / total, 0.0)
        block = iota((snaps, LANES), 1) // snaps
        steps = SUB // part

        def gram(h):
            rows = []
            for u in range(steps):
                at = pl.multiple_of((h * steps + u) * LANES, LANES)
                z = zbuf[pl.ds(at, LANES), :]
                zh, zl = halves(z)
                g4 = dot(left_terms(z * weight), jnp.concatenate([zh, zl, zh], axis=1), (((1,), (1,)), ((), ())))
                r = g4[:snaps]
                for b in range(1, pack):
                    r = jnp.where(block == b, g4[b * snaps:(b + 1) * snaps], r)
                rows.append(r)
            at = pl.multiple_of(h * SUB, SUB)
            for g in range(n_grp):
                new = jnp.concatenate([r[g * part:(g + 1) * part] for r in rows], axis=0)
                to = g // n_role % 2 * near + g // n_role // 2 * n_role + g % n_role
                if j == 0:
                    acc[to, pl.ds(at, SUB), :] = new
                else:
                    acc[to, pl.ds(at, SUB), :] += new

        count = modes // pack // steps // STAGES
        for t in range(STAGES):
            pl.loop(t * count, (t + 1) * count, unroll=UNROLL)(gram)
            if j == subs - 1:
                pair(t).start()
                if t > 0:
                    forward(t - 1)

    def last(s, slot):
        return pltpu.make_async_remote_copy(
            src_ref=sb.at[s], dst_ref=redb.at[slot],
            send_sem=sb_sem.at[s], recv_sem=rb_sem.at[slot],
            device_id={"sec": s}, device_id_type=MESH)

    forward(STAGES - 1)
    rows = sb.shape[1]
    for t in range(STAGES):
        for o in range(1, near):
            share(o, t, True).wait_recv()
        for s in range(t * n_sec // STAGES, (t + 1) * n_sec // STAGES):
            value = pacc[mine, s * rows:(s + 1) * rows, :]
            for o in range(1, near):
                value += reda[lax.rem(mine + o, near), s * rows:(s + 1) * rows, :]
            sb[s] = value

            @pl.when(me != s)
            def _():
                last(s, me).start()

    value = sb[me]
    for o in range(1, n_sec):
        s = lax.rem(me + o, n_sec)
        last(s, s).wait_recv()
        value += redb[s]
    out_ref[...] = value

    for j in range(subs):
        @pl.loop(1, n_sec)
        def _(i):
            outgoing(i, j).wait_send()
    for t in range(STAGES):
        pair(t).wait_send()
        for o in range(1, near):
            share(o, t).wait_send()
    for o in range(1, n_sec):
        last(lax.rem(me + o, n_sec), me).wait_send()


def on_device(pressure, cell_weight, live_cells, mode_order):
    n_sec, n_tile, n_role = (lax.axis_size(a) for a in ("sec", "tile", "role"))
    n_grp = n_tile * n_role
    snaps, q_loc, cells = pressure.shape
    modes = mode_order.shape[0]
    angles = q_loc * n_sec
    subs = cells // n_sec // LANES
    pack = LANES // snaps
    part = snaps // n_grp
    rows = modes // pack * part
    own_rows = rows // n_sec
    vmem = pl.BlockSpec(memory_space=pltpu.VMEM)
    dma = pltpu.SemaphoreType.DMA
    packed = pl.pallas_call(
        functools.partial(kernel, n_sec, n_tile, n_role),
        out_shape=jax.ShapeDtypeStruct((own_rows, LANES), F32),
        in_specs=[pl.BlockSpec(memory_space=pl.ANY), vmem, pl.BlockSpec(memory_space=pltpu.SMEM), vmem],
        out_specs=vmem,
        scratch_shapes=[
            pltpu.VMEM((subs, n_sec, snaps, q_loc, LANES), F32),
            pltpu.VMEM((snaps, angles, LANES), F32),
            pltpu.VMEM((modes * snaps, LANES), F32),
            pltpu.VMEM((n_grp, rows, LANES), F32),
            pltpu.VMEM((n_grp // 2, rows, LANES), F32),
            pltpu.VMEM((n_grp // 2, rows, LANES), F32),
            pltpu.VMEM((n_grp // 2, rows, LANES), F32),
            pltpu.VMEM((n_sec, own_rows, LANES), F32),
            pltpu.VMEM((n_sec, own_rows, LANES), F32),
            pltpu.VMEM((snaps * SUB, 3 * snaps * SUB), BF16),
            pltpu.VMEM((2 * modes, 3 * angles), BF16),
            pltpu.VMEM((2 * modes, 3 * q_loc), BF16),
            pltpu.VMEM((snaps // 2, 2 * modes, 2 * LANES), F32),
            dma((subs, n_sec)), dma((subs, n_sec)), dma((subs,)),
            dma((STAGES,)), dma((STAGES,)), dma((STAGES, n_grp // 2)), dma((STAGES, n_grp // 2)), dma((n_sec,)), dma((n_sec,)),
        ],
        compiler_params=pltpu.CompilerParams(
            collective_id=0, has_side_effects=True, vmem_limit_bytes=60 * 2**20),
        name="spod",
    )(pressure, cell_weight.reshape(cells // LANES, LANES), live_cells, mode_order.reshape(1, modes))
    out = packed.reshape(modes // pack // n_sec, part, pack, snaps)
    return out.transpose(0, 2, 1, 3).reshape(modes // n_sec, part, snaps)


def solution(mesh):
    in_specs = (P(None, "sec", ("tile", "role")), P(("tile", "role")), P(), P())
    out_specs = P("sec", ("tile", "role"), None)
    return jax.shard_map(
        on_device, mesh=mesh, in_specs=in_specs, out_specs=out_specs, check_vma=False
    )
```
